128 devices in a mesh: row: 32 (over z_lo, x, y), pair: 4 (over z_hi, core).
Axes of the slice: x: 4, y: 4, z: 4 (z_hi: 2, z_lo: 2; z = z_hi * 2 + z_lo), core: 2. Of those that a mesh axis runs over, the one named last changes fastest.
Arguments:
- snapshots: float32 [512, 4, 16384], P('row', 'pair'), may hold values from -6 to 6
- plan: int32 [2, 8], replicated, may hold values from 0 to 7, each once within a row
Outputs:
- rotated: float32 [512, 4, 16384], P(None, 'pair', 'row')
The draws below stay inside these ranges and needn't reach their ends.
Inputs may be any that keep to these rules, and one draw needn't show every extreme that they name: Each row of plan names every block once.
All inputs are finite; a program needn't handle non-finite values.
Results may differ from the reference program's by a relative error of at most 0.00013.
Values sent between devices are 32-bit elements; how exact they have to be, the bound alone decides.
A program may use at most 128 MiB of HBM per device.

```python
import jax
import jax.numpy as jnp
from jax import lax

ORDER = 512
ROWS = 16384
STEPS = 2
N_PAIR = 4


def block_levels(stream_key, extent, shards, least, high):
    loudness = 1.0
    for axis_at, shards_of in shards:
        heights = jax.random.uniform(jax.random.fold_in(jax.random.fold_in(stream_key, 6), axis_at), (shards_of,), jnp.float32, least / len(shards), high / len(shards))
        loudness = loudness * jnp.repeat(jnp.exp(heights), extent[axis_at] // shards_of).reshape((-1,) + (1,) * (len(extent) - 1 - axis_at))
    return loudness


def gaussian(own_key, dims, width, bound, shards=(), kind=jnp.bfloat16):
    gain = block_levels(own_key, dims, shards, -0.22, 0.18) if shards else 1.0
    array = jax.random.normal(own_key, dims, jnp.float32) * width * gain
    return jnp.minimum(jnp.maximum(array, -bound), bound).astype(kind)


def setup_inputs(seed: int = 0) -> dict:
    arg_keys = jax.random.split(jax.random.key(seed), 3)
    return {
        "snapshots": gaussian(arg_keys[0], (ORDER, N_PAIR, ROWS), 1.0, 6.0, ((0, 32), (1, 4)), jnp.float32),
        "plan": jax.vmap(lambda own: jax.random.permutation(own, 2 * N_PAIR))(jax.random.split(arg_keys[1], STEPS)).reshape((STEPS, 2 * N_PAIR)).astype(jnp.int32),
    }


def matmul(left, right):
    return jnp.dot(left.astype(jnp.float32), right.astype(jnp.float32), precision=lax.Precision.HIGHEST, preferred_element_type=jnp.float32)

def cayley(scaled):
    order_size = scaled.shape[0]
    identity = jnp.eye(order_size, dtype=jnp.float32)
    system = identity + matmul(scaled.T, scaled)
    lifted = identity + scaled
    square = matmul(lifted, lifted)
    lower = lax.linalg.cholesky(system)
    middle = lax.linalg.triangular_solve(lower, square, left_side=True, lower=True)
    return lax.linalg.triangular_solve(lower, middle, left_side=True, lower=True, transpose_a=True)

def rotation(gram):
    order_size = gram.shape[0]
    scales = lax.rsqrt(jnp.diagonal(gram))
    normed = gram * scales[:, None] * scales[None, :]
    column_ids = jnp.arange(order_size, dtype=jnp.int32)
    signs = jnp.sign(column_ids[None, :] - column_ids[:, None]).astype(jnp.float32)
    skew = normed * signs
    factor = 1.0 + jnp.sqrt(jnp.sum(skew * skew))
    return cayley(skew / factor)

def rotate_pair(pair_block):
    gram = matmul(pair_block, pair_block.T)
    return matmul(rotation(gram).T, pair_block)

def reference(snapshots, plan):
    order_size = snapshots.shape[0]
    pair_count = snapshots.shape[1]
    rows_all = snapshots.shape[2]
    block_width = order_size // 2
    blocks = jnp.transpose(snapshots, (1, 0, 2)).reshape(2 * pair_count, block_width, rows_all)
    for round_index in range(STEPS):
        placing = plan[round_index]
        arranged = blocks[placing].reshape(pair_count, order_size, rows_all)
        turned = lax.map(rotate_pair, arranged)
        blocks = jnp.zeros_like(blocks).at[placing].set(turned.reshape(2 * pair_count, block_width, rows_all))
    return jnp.transpose(blocks.reshape(pair_count, order_size, rows_all), (1, 0, 2))
```

```python
import functools

import jax
import jax.numpy as jnp
from jax import lax
from jax.experimental import pallas as pl
from jax.experimental.pallas import tpu as pltpu
from jax.sharding import PartitionSpec as P

MESH = pl.DeviceIdType.MESH
F32 = jnp.float32
BF16 = jnp.bfloat16
NN = (((1,), (0,)), ((), ()))
NT = (((1,), (1,)), ((), ()))
TILES = [(i, j) for i in range(4) for j in range(i, 4)]
TILE_ROWS = 128 * len(TILES)
T2_AT, T4_AT, T8_AT = 49.0, 4801.0, 46099201.0
INVERSE_SCALE = 32.0 * 5.0 * T2_AT * T4_AT / T8_AT


def dot(left, right, dims=NN):
    return lax.dot_general(left, right, dims, preferred_element_type=F32)


def split(value):
    high = value.astype(BF16)
    return high, (value - high.astype(F32)).astype(BF16)


def dot3(left, right, dims=NN):
    (left_high, left_low), (right_high, right_low) = left, right
    return (
        dot(left_high, right_high, dims)
        + dot(left_high, right_low, dims)
        + dot(left_low, right_high, dims)
    )


def identity(size):
    shape = (size, size)
    return lax.broadcasted_iota(jnp.int32, shape, 0) == lax.broadcasted_iota(jnp.int32, shape, 1)


def kernel(n_row, table, snap, out, S0, S1, S2, E, RSB, RED, G, f0, f1, h0, l0, h1, l1, h2, l2, h3,
           sem_in, sem_in_s, sem_sw, sem_sw_s, sem_rs, sem_rs_s, sem_ag, sem_ag_s):
    r = lax.axis_index("row")
    p = lax.axis_index("pair")
    h, c = p // 2, p % 2
    n_peer = 2 * n_row
    me = h * n_row + r
    part = TILE_ROWS // n_row
    order = 512
    half = 256
    S = (S0, S1, S2)
    width = S0.shape[2]
    own = snap.shape[0]
    partner = (r, 2 * h + 1 - c)

    def peer_of(k):
        peer = lax.rem(me + k, n_peer)
        return lax.rem(peer, n_row), peer // n_row

    barrier = pltpu.get_barrier_semaphore()

    def greet(k, carry):
        pr, ph = peer_of(k)
        pl.semaphore_signal(barrier, inc=1, device_id=(pr, 2 * ph + c), device_id_type=MESH)
        return carry

    pl.semaphore_signal(barrier, inc=1, device_id=partner, device_id_type=MESH)
    lax.fori_loop(1, n_peer, greet, 0)
    pl.semaphore_wait(barrier, n_peer)

    mine = S0.at[2 * p + (own * r) // half, pl.ds(pl.multiple_of(lax.rem(own * r, half), own), own), :]
    local = pltpu.make_async_copy(
        snap.at[:, 0, pl.ds(pl.multiple_of(width * r, width), width)], mine, sem_in.at[h])
    local.start()

    def scatter(k, carry):
        pr, ph = peer_of(k)
        pltpu.make_async_remote_copy(
            src_ref=snap.at[:, 0, pl.ds(pl.multiple_of(width * pr, width), width)],
            dst_ref=mine,
            send_sem=sem_in_s, recv_sem=sem_in.at[h],
            device_id=(pr, 2 * ph + c), device_id_type=MESH).start()
        return carry

    lax.fori_loop(1, n_peer, scatter, 0)

    def blocks_of(s, q):
        return S[s].at[pl.ds(2 * q, 2)]

    def swap(s, hq):
        q = 2 * hq + c
        return pltpu.make_async_remote_copy(
            src_ref=blocks_of(s, q), dst_ref=blocks_of(s, q),
            send_sem=sem_sw_s.at[s, hq], recv_sem=sem_sw.at[s, hq],
            device_id=partner, device_id_type=MESH)

    def await_bytes(ref, sem):
        pltpu.make_async_copy(ref, ref, sem).wait()

    def await_swap(s):
        for hq in range(2):
            other = blocks_of(s, 2 * hq + 1 - c)
            await_bytes(other, sem_sw.at[s, hq])
            await_bytes(other, sem_sw_s.at[s, hq])

    for hq in range(2):
        await_bytes(blocks_of(0, 2 * hq + c), sem_in.at[hq])
        swap(0, hq).start()
    await_bytes(S0.at[pl.ds(0, 6), pl.ds(0, own * (n_peer - 1) // 6), :], sem_in_s)
    await_swap(0)

    eye = identity(order)

    def load_pair(s, q):
        parts = [S[s][table[s, 2 * q + side]] for side in range(2)]
        return split(jnp.concatenate(parts, axis=0))

    def one_round(s):
        h0[...], l0[...] = load_pair(s, p)
        pair = (h0[...], l0[...])
        gram = dot3(pair, pair, NT)
        for n, (i, j) in enumerate(TILES):
            E[s, pl.ds(128 * n, 128), :] = gram[128 * i:128 * i + 128, 128 * j:128 * j + 128]

        def slice_of(k):
            return pl.ds(pl.multiple_of(part * k, part), part)

        def reduce_send(k, c2):
            pr = lax.rem(r + k, n_row)
            pltpu.make_async_remote_copy(
                src_ref=E.at[s, slice_of(pr), :], dst_ref=RSB.at[s, slice_of(r), :],
                send_sem=sem_rs_s.at[s], recv_sem=sem_rs.at[s],
                device_id=(pr, p), device_id_type=MESH).start()
            return c2

        pltpu.make_async_copy(E.at[s, slice_of(r), :], RSB.at[s, slice_of(r), :], sem_rs.at[s]).start()
        lax.fori_loop(1, n_row, reduce_send, 0)
        await_bytes(RSB.at[s], sem_rs.at[s])
        total = jnp.zeros((part, 128), F32)
        for k in range(n_row):
            total = total + RSB[s, pl.ds(part * k, part), :]
        RED[s] = total
        await_bytes(E.at[s, pl.ds(0, part * (n_row - 1)), :], sem_rs_s.at[s])

        def gather_send(k, c2):
            pr, ph = peer_of(k)
            pltpu.make_async_remote_copy(
                src_ref=RED.at[s], dst_ref=G.at[s, slice_of(h * n_row + r), :],
                send_sem=sem_ag_s.at[s], recv_sem=sem_ag.at[s, h],
                device_id=(pr, 2 * ph + c), device_id_type=MESH).start()
            return c2

        pltpu.make_async_copy(RED.at[s], G.at[s, slice_of(h * n_row + r), :], sem_ag.at[s, h]).start()
        lax.fori_loop(1, n_peer, gather_send, 0)

        def rotate(hq, c2):
            base = pl.multiple_of(TILE_ROWS * hq, TILE_ROWS)
            await_bytes(G.at[s, pl.ds(base, TILE_ROWS), :], sem_ag.at[s, hq])
            tile = {ij: G[s, pl.ds(base + 128 * n, 128), :] for n, ij in enumerate(TILES)}
            on = identity(128)
            columns, rows = [], []
            for i in range(4):
                diagonal = jnp.where(on, tile[i, i], 0.0)
                columns.append(lax.rsqrt(jnp.sum(diagonal, axis=1, keepdims=True)))
                rows.append(lax.rsqrt(jnp.sum(diagonal, axis=0, keepdims=True)))
            row_ids = lax.broadcasted_iota(jnp.int32, (128, 128), 0)
            column_ids = lax.broadcasted_iota(jnp.int32, (128, 128), 1)
            signs = jnp.where(column_ids > row_ids, 1.0, jnp.where(column_ids < row_ids, -1.0, 0.0))
            squares = jnp.zeros((128, 128), F32)
            skew = {}
            for i, j in TILES:
                normed = tile[i, j] * columns[i] * rows[j]
                if i == j:
                    normed = normed * signs
                    squares = squares + normed * normed
                else:
                    squares = squares + 2.0 * (normed * normed)
                skew[i, j] = normed
            scale = 1.0 / (1.0 + jnp.sqrt(jnp.sum(squares, keepdims=True)))
            for i, j in TILES:
                scaled = skew[i, j] * scale
                f0[pl.ds(128 * i, 128), pl.ds(128 * j, 128)] = scaled
                if i != j:
                    f0[pl.ds(128 * j, 128), pl.ds(128 * i, 128)] = -scaled.T
            h0[...], l0[...] = split(f0[...])
            a = (h0[...], l0[...])
            f1[...] = 4.0 * dot3(a, a) + jnp.where(eye, 1.0, 0.0)
            h1[...], l1[...] = split(f1[...])
            w = (h1[...], l1[...])
            h2[...], l2[...] = split(2.0 * dot3(w, w) - jnp.where(eye, 1.0, 0.0))
            t2 = (h2[...], l2[...])
            h3[...] = (2.0 * dot(h2[...], h2[...]) - jnp.where(eye, 1.0, 0.0)).astype(BF16)
            f0[...] = jnp.where(eye, 1.0, 0.0) - f0[...] + 0.2 * (f1[...] - dot3(a, w))
            h0[...], l0[...] = split(f0[...])
            f0[...] = f0[...] + (1.0 / T2_AT) * dot3((h0[...], l0[...]), t2)
            h0[...] = f0[...].astype(BF16)
            f0[...] = f0[...] + (1.0 / T4_AT) * dot(h0[...], h3[...])
            h0[...], l0[...] = split((2.0 * INVERSE_SCALE) * f0[...] - jnp.where(eye, 1.0, 0.0))
            q = 2 * hq + c
            h1[...], l1[...] = load_pair(s, q)
            turned = dot3((h0[...], l0[...]), (h1[...], l1[...]))
            for side in range(2):
                S[s + 1][2 * q + side] = turned[half * side:half * side + half]
            swap(s + 1, hq).start()
            return c2

        lax.fori_loop(0, 2, rotate, 0)
        await_bytes(G.at[s, pl.ds(0, part * (n_peer - 1)), :], sem_ag_s.at[s])
        await_swap(s + 1)

    one_round(0)
    one_round(1)
    for side in range(2):
        out[pl.ds(half * side, half), :] = S2[table[2, 2 * p + side]]


def places(plan):
    natural = jnp.arange(plan.shape[1], dtype=jnp.int32)
    wanted = jnp.stack([plan[1], natural])
    hits = plan[:, None, :] == wanted[:, :, None]
    found = jnp.sum(jnp.where(hits, natural, 0), axis=2)
    return jnp.concatenate([plan[:1], found], axis=0)


def on_device(n_row, snapshots, plan):
    width = snapshots.shape[2] // n_row
    part = TILE_ROWS // n_row
    dma = pltpu.SemaphoreType.DMA
    full = (512, 512)
    result = pl.pallas_call(
        functools.partial(kernel, n_row),
        out_shape=jax.ShapeDtypeStruct((512, width), F32),
        in_specs=[pl.BlockSpec(memory_space=pltpu.SMEM), pl.BlockSpec(memory_space=pl.ANY)],
        out_specs=pl.BlockSpec(memory_space=pltpu.VMEM),
        scratch_shapes=[
            pltpu.VMEM((8, 256, width), F32), pltpu.VMEM((8, 256, width), F32), pltpu.VMEM((8, 256, width), F32),
            pltpu.VMEM((2, TILE_ROWS, 128), F32),
            pltpu.VMEM((2, TILE_ROWS, 128), F32),
            pltpu.VMEM((2, part, 128), F32),
            pltpu.VMEM((2, 2 * TILE_ROWS, 128), F32),
            pltpu.VMEM(full, F32), pltpu.VMEM(full, F32),
            pltpu.VMEM(full, BF16), pltpu.VMEM(full, BF16), pltpu.VMEM(full, BF16), pltpu.VMEM(full, BF16),
            pltpu.VMEM(full, BF16), pltpu.VMEM(full, BF16), pltpu.VMEM(full, BF16),
            dma((2,)), dma, dma((3, 2)), dma((3, 2)), dma((2,)), dma((2,)), dma((2, 2)), dma((2,)),
        ],
        compiler_params=pltpu.CompilerParams(
            collective_id=0, has_side_effects=True, vmem_limit_bytes=60 * 1024 * 1024),
    )(places(plan), snapshots)
    return result[:, None, :]


def solution(mesh):
    n_row = mesh.shape["row"]
    return jax.shard_map(
        functools.partial(on_device, n_row), mesh=mesh,
        in_specs=(P("row", "pair", None), P()), out_specs=P(None, "pair", "row"), check_vma=False)
```

```python
import functools

import jax
import jax.numpy as jnp
from jax import lax
from jax.experimental import pallas as pl
from jax.experimental.pallas import tpu as pltpu
from jax.sharding import PartitionSpec as P

MESH = pl.DeviceIdType.MESH
F32 = jnp.float32
BF16 = jnp.bfloat16
NN = (((1,), (0,)), ((), ()))
NT = (((1,), (1,)), ((), ()))
TILES = [(i, j) for i in range(4) for j in range(i, 4)]
TILE_ROWS = 128 * len(TILES)
PIECES = (16, 16, 8)
T2_AT, T4_AT, T8_AT = 49.0, 4801.0, 46099201.0
INVERSE_SCALE = 32.0 * 5.0 * T2_AT * T4_AT / T8_AT


def dot(left, right, dims=NN):
    return lax.dot_general(left, right, dims, preferred_element_type=F32)


def chunk(at, size):
    return pl.ds(pl.multiple_of(size * at, size), size)


def split(value):
    high = value.astype(BF16)
    return high, (value - high.astype(F32)).astype(BF16)


def dot3(left, right, dims=NN):
    (left_high, left_low), (right_high, right_low) = left, right
    return (
        dot(left_high, right_high, dims)
        + dot(left_high, right_low, dims)
        + dot(left_low, right_high, dims)
    )


def identity(size):
    shape = (size, size)
    return lax.broadcasted_iota(jnp.int32, shape, 0) == lax.broadcasted_iota(jnp.int32, shape, 1)


def kernel(n_row, plan, snap, out, S0, S1, S2, E, RSB, G0, G1, G2, T, f0, f1, h0, l0, h1, l1, h2, l2, h3,
           sem_in, sem_in_s, sem_sw, sem_sw_s, sem_rs, sem_rs_s, sem_ag, sem_ag_s):
    r = lax.axis_index("row")
    p = lax.axis_index("pair")
    h, c = p // 2, p % 2
    n_peer = 2 * n_row
    me = h * n_row + r
    part = TILE_ROWS // n_row
    order = 512
    half = 256
    S = (S0, S1, S2)
    G = (G0, G1, G2)
    width = S0.shape[2]
    own = snap.shape[0]
    partner = (r, 2 * h + 1 - c)

    zl, x, y = r // 16, lax.rem(r // 4, 4), lax.rem(r, 4)
    z = 2 * h + zl

    def device(dx, dy, dz):
        px, py, pz = lax.rem(x + dx, 4), lax.rem(y + dy, 4), lax.rem(z + dz, 4)
        return 16 * lax.rem(pz, 2) + 4 * px + py, 2 * (pz // 2) + c

    def peer_of(k):
        k = lax.rem(37 * k, n_peer)
        return device(lax.rem(k // 4, 4), lax.rem(k, 4), k // 16)

    barrier = pltpu.get_barrier_semaphore()

    def greet(k, carry):
        pl.semaphore_signal(barrier, inc=1, device_id=peer_of(k), device_id_type=MESH)
        return carry

    pl.semaphore_signal(barrier, inc=1, device_id=partner, device_id_type=MESH)
    lax.fori_loop(1, n_peer, greet, 0)
    pl.semaphore_wait(barrier, n_peer)

    mine = S0.at[2 * p + (own * r) // half, pl.ds(pl.multiple_of(lax.rem(own * r, half), own), own), :]
    local = pltpu.make_async_copy(
        snap.at[:, 0, pl.ds(pl.multiple_of(width * r, width), width)], mine, sem_in.at[h])
    local.start()

    def scatter(k, carry):
        pr, pp = peer_of(k)
        pltpu.make_async_remote_copy(
            src_ref=snap.at[:, 0, pl.ds(pl.multiple_of(width * pr, width), width)],
            dst_ref=mine,
            send_sem=sem_in_s, recv_sem=sem_in.at[h],
            device_id=(pr, pp), device_id_type=MESH).start()
        return carry

    lax.fori_loop(1, n_peer, scatter, 0)

    def blocks_of(s, q):
        return S[s].at[pl.ds(2 * q, 2)]

    def swap(s, hq):
        q = 2 * hq + c
        return pltpu.make_async_remote_copy(
            src_ref=blocks_of(s, q), dst_ref=blocks_of(s, q),
            send_sem=sem_sw_s.at[s, hq], recv_sem=sem_sw.at[s, hq],
            device_id=partner, device_id_type=MESH)

    def await_bytes(ref, sem):
        pltpu.make_async_copy(ref, ref, sem).wait()

    def await_swap(s):
        for hq in range(2):
            other = blocks_of(s, 2 * hq + 1 - c)
            await_bytes(other, sem_sw.at[s, hq])
            await_bytes(other, sem_sw_s.at[s, hq])

    for hq in range(2):
        await_bytes(blocks_of(0, 2 * hq + c), sem_in.at[hq])
        swap(0, hq).start()
    await_bytes(S0.at[pl.ds(0, 6), pl.ds(0, own * (n_peer - 1) // 6), :], sem_in_s)
    await_swap(0)

    eye = identity(order)

    def place(round_at, block):
        at = jnp.int32(0)
        for k in range(1, 8):
            at = at + k * (plan[round_at, k] == block).astype(jnp.int32)
        return jnp.minimum(at, 7)

    def load_pair(s, q):
        wanted = [plan[s, 2 * q + side] for side in range(2)]
        parts = [S[s][block if s == 0 else place(0, block)] for block in wanted]
        return split(jnp.concatenate(parts, axis=0))

    def one_round(s):
        h0[...], l0[...] = load_pair(s, p)
        pair = (h0[...], l0[...])
        gram = dot3(pair, pair, NT)
        for n, (i, j) in enumerate(TILES):
            E[s, pl.ds(128 * n, 128), :] = gram[128 * i:128 * i + 128, 128 * j:128 * j + 128]

        def slice_of(k):
            return pl.ds(pl.multiple_of(part * k, part), part)

        def reduce_send(k, c2):
            k = lax.rem(21 * k, n_row)
            pr = 16 * lax.rem(zl + k // 16, 2) + 4 * lax.rem(x + k // 4, 4) + lax.rem(y + k, 4)
            pltpu.make_async_remote_copy(
                src_ref=E.at[s, slice_of(pr), :], dst_ref=RSB.at[s, slice_of(r), :],
                send_sem=sem_rs_s.at[s], recv_sem=sem_rs.at[s],
                device_id=(pr, p), device_id_type=MESH).start()
            return c2

        pltpu.make_async_copy(E.at[s, slice_of(r), :], RSB.at[s, slice_of(r), :], sem_rs.at[s]).start()
        lax.fori_loop(1, n_row, reduce_send, 0)
        await_bytes(RSB.at[s], sem_rs.at[s])
        total = jnp.zeros((part, 128), F32)
        for k in range(n_row):
            total = total + RSB[s, pl.ds(part * k, part), :]
        own_at = (16 * x + 4 * z + y, 16 * y + 4 * z + x, 16 * z + 4 * x + y)
        line_at = (x, y, z)
        first = 0
        for colour, size in enumerate(PIECES):
            G[colour][s, chunk(own_at[colour], size), :] = total[first:first + size]
            first += size

        def plane_send(k, c2):
            k = lax.rem(7 * k, 16)
            near, far = lax.rem(k, 4), k // 4
            targets = (device(0, near, far), device(near, 0, far), device(far, near, 0))
            for colour, size in enumerate(PIECES):
                piece = G[colour].at[s, chunk(own_at[colour], size), :]
                pltpu.make_async_remote_copy(
                    src_ref=piece, dst_ref=piece,
                    send_sem=sem_ag_s.at[s, colour, 0], recv_sem=sem_ag.at[s, colour, 0],
                    device_id=targets[colour], device_id_type=MESH).start()
            return c2

        lax.fori_loop(1, 16, plane_send, 0)
        await_bytes(E.at[s, pl.ds(0, part * (n_row - 1)), :], sem_rs_s.at[s])
        for colour, size in enumerate(PIECES):
            await_bytes(G[colour].at[s, pl.ds(0, 15 * size), :], sem_ag.at[s, colour, 0])
            line = G[colour].at[s, chunk(line_at[colour], 16 * size), :]
            for k in (2, 1, 3):
                pltpu.make_async_remote_copy(
                    src_ref=line, dst_ref=line,
                    send_sem=sem_ag_s.at[s, colour, 1], recv_sem=sem_ag.at[s, colour, 1],
                    device_id=(device(k, 0, 0), device(0, k, 0), device(0, 0, k))[colour],
                    device_id_type=MESH).start()
        for colour, size in enumerate(PIECES):
            await_bytes(G[colour].at[s, pl.ds(0, 48 * size), :], sem_ag.at[s, colour, 1])

        def rotate(hq, c2):
            for k in range(n_row):
                kz, kx, ky = 2 * hq + k // 16, (k // 4) % 4, k % 4
                first = part * k
                for colour, size in enumerate(PIECES):
                    at = (16 * kx + 4 * kz + ky, 16 * ky + 4 * kz + kx, 16 * kz + 4 * kx + ky)[colour]
                    T[pl.ds(first, size), :] = G[colour][s, chunk(at, size), :]
                    first += size
            tile = {ij: T[pl.ds(128 * n, 128), :] for n, ij in enumerate(TILES)}
            on = identity(128)
            columns, rows = [], []
            for i in range(4):
                diagonal = jnp.where(on, tile[i, i], 0.0)
                columns.append(lax.rsqrt(jnp.sum(diagonal, axis=1, keepdims=True)))
                rows.append(lax.rsqrt(jnp.sum(diagonal, axis=0, keepdims=True)))
            row_ids = lax.broadcasted_iota(jnp.int32, (128, 128), 0)
            column_ids = lax.broadcasted_iota(jnp.int32, (128, 128), 1)
            signs = jnp.where(column_ids > row_ids, 1.0, jnp.where(column_ids < row_ids, -1.0, 0.0))
            squares = jnp.zeros((128, 128), F32)
            skew = {}
            for i, j in TILES:
                normed = tile[i, j] * columns[i] * rows[j]
                if i == j:
                    normed = normed * signs
                    squares = squares + normed * normed
                else:
                    squares = squares + 2.0 * (normed * normed)
                skew[i, j] = normed
            scale = 1.0 / (1.0 + jnp.sqrt(jnp.sum(squares, keepdims=True)))
            for i, j in TILES:
                scaled = skew[i, j] * scale
                f0[pl.ds(128 * i, 128), pl.ds(128 * j, 128)] = scaled
                if i != j:
                    f0[pl.ds(128 * j, 128), pl.ds(128 * i, 128)] = -scaled.T
            h0[...], l0[...] = split(f0[...])
            a = (h0[...], l0[...])
            f1[...] = 4.0 * dot3(a, a) + jnp.where(eye, 1.0, 0.0)
            h1[...], l1[...] = split(f1[...])
            w = (h1[...], l1[...])
            h2[...], l2[...] = split(2.0 * dot3(w, w) - jnp.where(eye, 1.0, 0.0))
            t2 = (h2[...], l2[...])
            h3[...] = (2.0 * dot(h2[...], h2[...]) - jnp.where(eye, 1.0, 0.0)).astype(BF16)
            f0[...] = jnp.where(eye, 1.0, 0.0) - f0[...] + 0.2 * (f1[...] - dot3(a, w))
            h0[...], l0[...] = split(f0[...])
            f0[...] = f0[...] + (1.0 / T2_AT) * dot3((h0[...], l0[...]), t2)
            h0[...] = f0[...].astype(BF16)
            f0[...] = f0[...] + (1.0 / T4_AT) * dot(h0[...], h3[...])
            h0[...], l0[...] = split((2.0 * INVERSE_SCALE) * f0[...] - jnp.where(eye, 1.0, 0.0))
            q = 2 * hq + c
            h1[...], l1[...] = load_pair(s, q)
            turned = dot3((h0[...], l0[...]), (h1[...], l1[...]))
            for side in range(2):
                S[s + 1][2 * q + side] = turned[half * side:half * side + half]
            swap(s + 1, hq).start()
            return c2

        lax.fori_loop(0, 2, rotate, 0)
        for colour, size in enumerate(PIECES):
            await_bytes(G[colour].at[s, pl.ds(0, 15 * size), :], sem_ag_s.at[s, colour, 0])
            await_bytes(G[colour].at[s, pl.ds(0, 48 * size), :], sem_ag_s.at[s, colour, 1])
        await_swap(s + 1)

    one_round(0)
    one_round(1)
    for side in range(2):
        out[pl.ds(half * side, half), :] = S2[place(1, 2 * p + side)]


def on_device(n_row, snapshots, plan):
    width = snapshots.shape[2] // n_row
    dma = pltpu.SemaphoreType.DMA
    full = (512, 512)
    result = pl.pallas_call(
        functools.partial(kernel, n_row),
        out_shape=jax.ShapeDtypeStruct((512, width), F32),
        in_specs=[pl.BlockSpec(memory_space=pltpu.SMEM), pl.BlockSpec(memory_space=pl.ANY)],
        out_specs=pl.BlockSpec(memory_space=pltpu.VMEM),
        scratch_shapes=[
            pltpu.VMEM((8, 256, width), F32), pltpu.VMEM((8, 256, width), F32), pltpu.VMEM((8, 256, width), F32),
            pltpu.VMEM((2, TILE_ROWS, 128), F32),
            pltpu.VMEM((2, TILE_ROWS, 128), F32),
            *[pltpu.VMEM((2, 64 * size, 128), F32) for size in PIECES],
            pltpu.VMEM((TILE_ROWS, 128), F32),
            pltpu.VMEM(full, F32), pltpu.VMEM(full, F32),
            pltpu.VMEM(full, BF16), pltpu.VMEM(full, BF16), pltpu.VMEM(full, BF16), pltpu.VMEM(full, BF16),
            pltpu.VMEM(full, BF16), pltpu.VMEM(full, BF16), pltpu.VMEM(full, BF16),
            dma((2,)), dma, dma((3, 2)), dma((3, 2)), dma((2,)), dma((2,)), dma((2, 3, 2)), dma((2, 3, 2)),
        ],
        compiler_params=pltpu.CompilerParams(
            collective_id=0, has_side_effects=True, vmem_limit_bytes=60 * 1024 * 1024),
    )(plan, snapshots)
    return result[:, None, :]


def solution(mesh):
    n_row = mesh.shape["row"]
    return jax.shard_map(
        functools.partial(on_device, n_row), mesh=mesh,
        in_specs=(P("row", "pair", None), P()), out_specs=P(None, "pair", "row"), check_vma=False)
```

```python
import functools

import jax
import jax.numpy as jnp
from jax import lax
from jax.experimental import pallas as pl
from jax.experimental.pallas import tpu as pltpu
from jax.sharding import PartitionSpec as P

MESH = pl.DeviceIdType.MESH
F32 = jnp.float32
BF16 = jnp.bfloat16
NN = (((1,), (0,)), ((), ()))
NT = (((1,), (1,)), ((), ()))
TILES = [(i, j) for i in range(4) for j in range(i, 4)]
TILE_ROWS = 128 * len(TILES)
PIECES = (16, 16, 8)


def dot(left, right, dims=NN):
    return lax.dot_general(left, right, dims, preferred_element_type=F32)


def chunk(at, size):
    return pl.ds(pl.multiple_of(size * at, size), size)


def split(value):
    high = value.astype(BF16)
    return high, (value - high.astype(F32)).astype(BF16)


def dot3(left, right, dims=NN):
    (left_high, left_low), (right_high, right_low) = left, right
    return (
        dot(left_high, right_high, dims)
        + dot(left_high, right_low, dims)
        + dot(left_low, right_high, dims)
    )


def identity(size):
    shape = (size, size)
    return lax.broadcasted_iota(jnp.int32, shape, 0) == lax.broadcasted_iota(jnp.int32, shape, 1)


def kernel(n_row, plan, snap, out, S0, S1, S2, E, B0, B1, B2, G0, G1, G2, T, f0, f1, h0, l0, h1, l1, h2, h3,
           sem_in, sem_in_s, sem_fw, sem_fw_s, sem_sw, sem_sw_s, sem_rs, sem_rs_s, sem_ag, sem_ag_s):
    r = lax.axis_index("row")
    p = lax.axis_index("pair")
    h, c = p // 2, p % 2
    n_peer = 2 * n_row
    me = h * n_row + r
    part = TILE_ROWS // n_row
    order = 512
    half = 256
    S = (S0, S1, S2)
    G = (G0, G1, G2)
    RSB = (B0, B1, B2)
    width = S0.shape[2]
    own = snap.shape[0]
    partner = (r, 2 * h + 1 - c)

    zl, x, y = r // 16, lax.rem(r // 4, 4), lax.rem(r, 4)
    z = 2 * h + zl

    def device(dx, dy, dz):
        px, py, pz = lax.rem(x + dx, 4), lax.rem(y + dy, 4), lax.rem(z + dz, 4)
        return 16 * lax.rem(pz, 2) + 4 * px + py, 2 * (pz // 2) + c

    def peer_of(k):
        k = lax.rem(37 * k, n_peer)
        return device(lax.rem(k // 4, 4), lax.rem(k, 4), k // 16)

    def source_of(k):
        k = lax.rem(37 * k, n_peer)
        return device(lax.rem(4 - k // 4 % 4, 4), lax.rem(4 - k % 4, 4), lax.rem(4 - k // 16, 4))

    barrier = pltpu.get_barrier_semaphore()

    def greet(k, carry):
        pl.semaphore_signal(barrier, inc=1, device_id=peer_of(k), device_id_type=MESH)
        return carry

    pl.semaphore_signal(barrier, inc=1, device_id=partner, device_id_type=MESH)
    lax.fori_loop(1, n_peer, greet, 0)
    pl.semaphore_wait(barrier, n_peer)

    def home(row_at, pair_at):
        first = own * row_at
        return S0.at[2 * pair_at + first // half, pl.ds(pl.multiple_of(lax.rem(first, half), own), own), :]

    def columns_for(row_at):
        return snap.at[:, 0, pl.ds(pl.multiple_of(width * row_at, width), width)]

    local = pltpu.make_async_copy(columns_for(r), home(r, p), sem_in.at[0])
    local.start()

    def scatter(k, carry):
        pr, pp = peer_of(k)
        pltpu.make_async_remote_copy(
            src_ref=columns_for(pr), dst_ref=home(r, p),
            send_sem=sem_in_s, recv_sem=sem_in.at[k],
            device_id=(pr, pp), device_id_type=MESH).start()
        return carry

    lax.fori_loop(1, n_peer, scatter, 0)

    def forward(k, carry):
        arrived = home(*source_of(k))
        await_bytes(arrived, sem_in.at[k])
        pltpu.make_async_remote_copy(
            src_ref=arrived, dst_ref=arrived, send_sem=sem_fw_s, recv_sem=sem_fw,
            device_id=partner, device_id_type=MESH).start()
        return carry

    def await_bytes(ref, sem):
        pltpu.make_async_copy(ref, ref, sem).wait()

    lax.fori_loop(0, n_peer, forward, 0)
    await_bytes(S0.at[pl.ds(0, 6), pl.ds(0, own * (n_peer - 1) // 6), :], sem_in_s)
    await_bytes(S0.at[pl.ds(0, 4)], sem_fw)
    await_bytes(S0.at[pl.ds(0, 4)], sem_fw_s)

    def blocks_of(s, q):
        return S[s].at[pl.ds(2 * q, 2)]

    def swap(s, hq):
        q = 2 * hq + c
        return pltpu.make_async_remote_copy(
            src_ref=blocks_of(s, q), dst_ref=blocks_of(s, q),
            send_sem=sem_sw_s.at[s - 1, hq], recv_sem=sem_sw.at[s - 1, hq],
            device_id=partner, device_id_type=MESH)

    def await_swap(s):
        for hq in range(2):
            other = blocks_of(s, 2 * hq + 1 - c)
            await_bytes(other, sem_sw.at[s - 1, hq])
            await_bytes(other, sem_sw_s.at[s - 1, hq])

    eye = identity(order)

    def place(round_at, block):
        at = jnp.int32(0)
        for k in range(1, 8):
            at = at + k * (plan[round_at, k] == block).astype(jnp.int32)
        return jnp.minimum(at, 7)

    def load_pair(s, q):
        wanted = [plan[s, 2 * q + side] for side in range(2)]
        parts = [S[s][block if s == 0 else place(0, block)] for block in wanted]
        return split(jnp.concatenate(parts, axis=0))

    def one_round(s):
        h0[...], l0[...] = load_pair(s, p)
        pair = (h0[...], l0[...])
        gram = dot3(pair, pair, NT)
        for n, (i, j) in enumerate(TILES):
            E[s, pl.ds(128 * n, 128), :] = gram[128 * i:128 * i + 128, 128 * j:128 * j + 128]

        own_at = (16 * x + 4 * z + y, 16 * y + 4 * z + x, 16 * z + 4 * x + y)
        line_at = (x, y, z)

        def piece_of(colour, k):
            first = part * k + sum(PIECES[:colour])
            return E.at[s, pl.ds(pl.multiple_of(first, 8), PIECES[colour]), :]

        for colour, size in enumerate(PIECES):
            def reduce_send(k, c2):
                k = lax.rem(21 * k, n_row)
                pr = 16 * lax.rem(zl + k // 16, 2) + 4 * lax.rem(x + k // 4, 4) + lax.rem(y + k, 4)
                pltpu.make_async_remote_copy(
                    src_ref=piece_of(colour, pr), dst_ref=RSB[colour].at[s, chunk(r, size), :],
                    send_sem=sem_rs_s.at[s, colour], recv_sem=sem_rs.at[s, colour],
                    device_id=(pr, p), device_id_type=MESH).start()
                return c2

            pltpu.make_async_copy(
                piece_of(colour, r), RSB[colour].at[s, chunk(r, size), :], sem_rs.at[s, colour]).start()
            lax.fori_loop(1, n_row, reduce_send, 0)

        for colour, size in enumerate(PIECES):
            await_bytes(RSB[colour].at[s], sem_rs.at[s, colour])
            total = jnp.zeros((size, 128), F32)
            for k in range(n_row):
                total = total + RSB[colour][s, pl.ds(size * k, size), :]
            G[colour][s, chunk(own_at[colour], size), :] = total

            def plane_send(k, c2):
                k = lax.rem(7 * k, 16)
                near, far = lax.rem(k, 4), k // 4
                target = (device(0, near, far), device(near, 0, far), device(far, near, 0))[colour]
                piece = G[colour].at[s, chunk(own_at[colour], size), :]
                pltpu.make_async_remote_copy(
                    src_ref=piece, dst_ref=piece,
                    send_sem=sem_ag_s.at[s, colour, 0], recv_sem=sem_ag.at[s, colour, 0],
                    device_id=target, device_id_type=MESH).start()
                return c2

            lax.fori_loop(1, 16, plane_send, 0)
        for colour, size in enumerate(PIECES):
            await_bytes(G[colour].at[s, pl.ds(0, 15 * size), :], sem_ag.at[s, colour, 0])
            line = G[colour].at[s, chunk(line_at[colour], 16 * size), :]
            for k in (2, 1, 3):
                pltpu.make_async_remote_copy(
                    src_ref=line, dst_ref=line,
                    send_sem=sem_ag_s.at[s, colour, 1], recv_sem=sem_ag.at[s, colour, 1],
                    device_id=(device(k, 0, 0), device(0, k, 0), device(0, 0, k))[colour],
                    device_id_type=MESH).start()
        for colour, size in enumerate(PIECES):
            await_bytes(G[colour].at[s, pl.ds(0, 48 * size), :], sem_ag.at[s, colour, 1])

        def rotate(hq, c2):
            for k in range(n_row):
                kz, kx, ky = 2 * hq + k // 16, (k // 4) % 4, k % 4
                first = part * k
                for colour, size in enumerate(PIECES):
                    at = (16 * kx + 4 * kz + ky, 16 * ky + 4 * kz + kx, 16 * kz + 4 * kx + ky)[colour]
                    T[pl.ds(first, size), :] = G[colour][s, chunk(at, size), :]
                    first += size
            tile = {ij: T[pl.ds(128 * n, 128), :] for n, ij in enumerate(TILES)}
            on = identity(128)
            columns, rows = [], []
            for i in range(4):
                diagonal = jnp.where(on, tile[i, i], 0.0)
                columns.append(lax.rsqrt(jnp.sum(diagonal, axis=1, keepdims=True)))
                rows.append(lax.rsqrt(jnp.sum(diagonal, axis=0, keepdims=True)))
            row_ids = lax.broadcasted_iota(jnp.int32, (128, 128), 0)
            column_ids = lax.broadcasted_iota(jnp.int32, (128, 128), 1)
            signs = jnp.where(column_ids > row_ids, 1.0, jnp.where(column_ids < row_ids, -1.0, 0.0))
            squares = jnp.zeros((128, 128), F32)
            skew = {}
            for i, j in TILES:
                normed = tile[i, j] * columns[i] * rows[j]
                if i == j:
                    normed = normed * signs
                    squares = squares + normed * normed
                else:
                    squares = squares + 2.0 * (normed * normed)
                skew[i, j] = normed
            scale = 1.0 / (1.0 + jnp.sqrt(jnp.sum(squares, keepdims=True)))
            for i, j in TILES:
                scaled = skew[i, j] * scale
                f0[pl.ds(128 * i, 128), pl.ds(128 * j, 128)] = scaled
                if i != j:
                    f0[pl.ds(128 * j, 128), pl.ds(128 * i, 128)] = -scaled.T
            h0[...], l0[...] = split(f0[...])
            square = dot(h0[...], h0[...])
            h1[...] = square.astype(BF16)
            f1[...] = (32.0 / 49.0) * square - (48.0 / 49.0) * f0[...] + jnp.where(eye, 48.0 / 49.0, 0.0)
            h2[...] = (f1[...] - (32.0 / 49.0) * dot(h0[...], h1[...])).astype(BF16)
            f0[...] = (
                jnp.where(eye, 1.0, 0.0) - h2[...].astype(F32) - (dot(h0[...], h2[...]) + dot(l0[...], h2[...])))
            h1[...] = f0[...].astype(BF16)
            square = dot(h1[...], h1[...])
            h3[...] = square.astype(BF16)
            h0[...], l0[...] = split(f0[...] + square)
            f0[...] = h2[...].astype(F32) + (dot(h2[...], h0[...]) + dot(h2[...], l0[...]))
            h2[...] = dot(h1[...], h3[...]).astype(BF16)
            h0[...] = f0[...].astype(BF16)
            inverse = f0[...] + dot(h0[...], h2[...])
            h0[...], l0[...] = split(2.0 * inverse - jnp.where(eye, 1.0, 0.0))
            q = 2 * hq + c
            h1[...], l1[...] = load_pair(s, q)
            turned = dot3((h0[...], l0[...]), (h1[...], l1[...]))
            for side in range(2):
                S[s + 1][2 * q + side] = turned[half * side:half * side + half]
            swap(s + 1, hq).start()
            return c2

        lax.fori_loop(0, 2, rotate, 0)
        for colour, size in enumerate(PIECES):
            await_bytes(RSB[colour].at[s, pl.ds(0, size * (n_row - 1)), :], sem_rs_s.at[s, colour])
            await_bytes(G[colour].at[s, pl.ds(0, 15 * size), :], sem_ag_s.at[s, colour, 0])
            await_bytes(G[colour].at[s, pl.ds(0, 48 * size), :], sem_ag_s.at[s, colour, 1])
        await_swap(s + 1)

    one_round(0)
    one_round(1)
    for side in range(2):
        out[pl.ds(half * side, half), :] = S2[place(1, 2 * p + side)]


def on_device(n_row, snapshots, plan):
    width = snapshots.shape[2] // n_row
    dma = pltpu.SemaphoreType.DMA
    full = (512, 512)
    result = pl.pallas_call(
        functools.partial(kernel, n_row),
        out_shape=jax.ShapeDtypeStruct((512, width), F32),
        in_specs=[pl.BlockSpec(memory_space=pltpu.SMEM), pl.BlockSpec(memory_space=pl.ANY)],
        out_specs=pl.BlockSpec(memory_space=pltpu.VMEM),
        scratch_shapes=[
            pltpu.VMEM((8, 256, width), F32), pltpu.VMEM((8, 256, width), F32), pltpu.VMEM((8, 256, width), F32),
            pltpu.VMEM((2, TILE_ROWS, 128), F32),
            *[pltpu.VMEM((2, n_row * size, 128), F32) for size in PIECES],
            *[pltpu.VMEM((2, 64 * size, 128), F32) for size in PIECES],
            pltpu.VMEM((TILE_ROWS, 128), F32),
            pltpu.VMEM(full, F32), pltpu.VMEM(full, F32),
            pltpu.VMEM(full, BF16), pltpu.VMEM(full, BF16), pltpu.VMEM(full, BF16), pltpu.VMEM(full, BF16),
            pltpu.VMEM(full, BF16), pltpu.VMEM(full, BF16),
            dma((2 * n_row,)), dma, dma, dma, dma((2, 2)), dma((2, 2)), dma((2, 3)), dma((2, 3)), dma((2, 3, 2)), dma((2, 3, 2)),
        ],
        compiler_params=pltpu.CompilerParams(
            collective_id=0, has_side_effects=True, vmem_limit_bytes=60 * 1024 * 1024),
    )(plan, snapshots)
    return result[:, None, :]


def solution(mesh):
    n_row = mesh.shape["row"]
    return jax.shard_map(
        functools.partial(on_device, n_row), mesh=mesh,
        in_specs=(P("row", "pair", None), P()), out_specs=P(None, "pair", "row"), check_vma=False)
```

```python
import functools

import jax
import jax.numpy as jnp
from jax import lax
from jax.experimental import pallas as pl
from jax.experimental.pallas import tpu as pltpu
from jax.sharding import PartitionSpec as P

MESH = pl.DeviceIdType.MESH
F32 = jnp.float32
BF16 = jnp.bfloat16
NN = (((1,), (0,)), ((), ()))
NT = (((1,), (1,)), ((), ()))
TILES = [(i, j) for i in range(4) for j in range(i + 1, 4)] + [(0, 0), (2, 2)]
TILE_ROWS = 128 * len(TILES)
PIECES = (8, 8, 16)
ORDER = [(2, PIECES[2]), (0, PIECES[0]), (1, PIECES[1])]


def dot(left, right, dims=NN):
    return lax.dot_general(left, right, dims, preferred_element_type=F32)


def chunk(at, size):
    return pl.ds(pl.multiple_of(size * at, size), size)


def split(value):
    high = value.astype(BF16)
    return high, (value - high.astype(F32)).astype(BF16)


def dot3(left, right, dims=NN):
    (left_high, left_low), (right_high, right_low) = left, right
    return (
        dot(left_high, right_high, dims)
        + dot(left_high, right_low, dims)
        + dot(left_low, right_high, dims)
    )


def identity(size):
    shape = (size, size)
    return lax.broadcasted_iota(jnp.int32, shape, 0) == lax.broadcasted_iota(jnp.int32, shape, 1)


def kernel(n_row, plan, snap, out, S0, S1, S2, E, B0, B1, B2, G0, G1, G2, T, D, DB, DS, f0, f1, h0, l0, h1, l1, h2, h3,
           sem_d, sem_d_s, sem_ds, sem_ds_s, sem_in, sem_in_s, sem_fw, sem_fw_s, sem_sw, sem_sw_s, sem_rs, sem_rs_s, sem_ag, sem_ag_s):
    r = lax.axis_index("row")
    p = lax.axis_index("pair")
    h, c = p // 2, p % 2
    n_peer = 2 * n_row
    me = h * n_row + r
    part = TILE_ROWS // n_row
    order = 512
    half = 256
    S = (S0, S1, S2)
    G = (G0, G1, G2)
    RSB = (B0, B1, B2)
    width = S0.shape[2]
    own = snap.shape[0]
    partner = (r, 2 * h + 1 - c)

    zl, x, y = r // 16, lax.rem(r // 4, 4), lax.rem(r, 4)
    z = 2 * h + zl

    def device(dx, dy, dz):
        px, py, pz = lax.rem(x + dx, 4), lax.rem(y + dy, 4), lax.rem(z + dz, 4)
        return 16 * lax.rem(pz, 2) + 4 * px + py, 2 * (pz // 2) + c

    def peer_of(k):
        k = lax.rem(37 * k, n_peer)
        return device(lax.rem(k // 4, 4), lax.rem(k, 4), k // 16)

    def source_of(k):
        k = lax.rem(37 * k, n_peer)
        return device(lax.rem(4 - k // 4 % 4, 4), lax.rem(4 - k % 4, 4), lax.rem(4 - k // 16, 4))

    barrier = pltpu.get_barrier_semaphore()

    def greet(k, carry):
        pl.semaphore_signal(barrier, inc=1, device_id=peer_of(k), device_id_type=MESH)
        return carry

    pl.semaphore_signal(barrier, inc=1, device_id=partner, device_id_type=MESH)
    lax.fori_loop(1, n_peer, greet, 0)
    pl.semaphore_wait(barrier, n_peer)

    def home(row_at, pair_at):
        first = own * row_at
        return S0.at[2 * pair_at + first // half, pl.ds(pl.multiple_of(lax.rem(first, half), own), own), :]

    def columns_for(row_at):
        return snap.at[:, 0, pl.ds(pl.multiple_of(width * row_at, width), width)]

    local = pltpu.make_async_copy(columns_for(r), home(r, p), sem_in.at[0])
    local.start()

    def scatter(k, carry):
        pr, pp = peer_of(k)
        pltpu.make_async_remote_copy(
            src_ref=columns_for(pr), dst_ref=home(r, p),
            send_sem=sem_in_s, recv_sem=sem_in.at[k],
            device_id=(pr, pp), device_id_type=MESH).start()
        return carry

    lax.fori_loop(1, n_peer, scatter, 0)

    def forward(k, carry):
        arrived = home(*source_of(k))
        await_bytes(arrived, sem_in.at[k])
        pltpu.make_async_remote_copy(
            src_ref=arrived, dst_ref=arrived, send_sem=sem_fw_s, recv_sem=sem_fw,
            device_id=partner, device_id_type=MESH).start()
        return carry

    def await_bytes(ref, sem):
        pltpu.make_async_copy(ref, ref, sem).wait()

    lax.fori_loop(0, n_peer, forward, 0)
    await_bytes(S0.at[pl.ds(0, 6), pl.ds(0, own * (n_peer - 1) // 6), :], sem_in_s)
    await_bytes(S0.at[pl.ds(0, 4)], sem_fw)
    await_bytes(S0.at[pl.ds(0, 4)], sem_fw_s)

    def blocks_of(s, q):
        return S[s].at[pl.ds(2 * q, 2)]

    def swap(s, hq):
        q = 2 * hq + c
        return pltpu.make_async_remote_copy(
            src_ref=blocks_of(s, q), dst_ref=blocks_of(s, q),
            send_sem=sem_sw_s.at[s - 1, hq], recv_sem=sem_sw.at[s - 1, hq],
            device_id=partner, device_id_type=MESH)

    def await_swap(s):
        for hq in range(2):
            other = blocks_of(s, 2 * hq + 1 - c)
            await_bytes(other, sem_sw.at[s - 1, hq])
            await_bytes(other, sem_sw_s.at[s - 1, hq])

    eye = identity(order)
    on = identity(128)
    row_ids = lax.broadcasted_iota(jnp.int32, (128, 128), 0)
    column_ids = lax.broadcasted_iota(jnp.int32, (128, 128), 1)
    D[...] = jnp.zeros_like(D)

    def place(round_at, block):
        at = jnp.int32(0)
        for k in range(1, 8):
            at = at + k * (plan[round_at, k] == block).astype(jnp.int32)
        return jnp.minimum(at, 7)

    def load_pair(s, q):
        wanted = [plan[s, 2 * q + side] for side in range(2)]
        parts = [S[s][block if s == 0 else place(0, block)] for block in wanted]
        return split(jnp.concatenate(parts, axis=0))

    def send_diagonal(s):
        @pl.when(r > 0)
        def _():
            pltpu.make_async_remote_copy(
                src_ref=D.at[s], dst_ref=DB.at[s, r], send_sem=sem_d_s.at[s], recv_sem=sem_d.at[s],
                device_id=(0, p), device_id_type=MESH).start()

    def sum_diagonal(s):
        @pl.when(r == 0)
        def _():
            await_bytes(DB.at[s, pl.ds(1, n_row - 1)], sem_d.at[s])
            total = D[s]
            for k in range(1, n_row):
                total = total + DB[s, k]
            DS[s, h] = total

            def send(k, carry):
                pltpu.make_async_remote_copy(
                    src_ref=DS.at[s, h], dst_ref=DS.at[s, h], send_sem=sem_ds_s.at[s], recv_sem=sem_ds.at[s, h],
                    device_id=peer_of(k), device_id_type=MESH).start()
                return carry

            lax.fori_loop(1, n_peer, send, 0)

    def await_diagonal(s):
        @pl.when(r > 0)
        def _():
            await_bytes(D.at[s], sem_d_s.at[s])
            await_bytes(DS.at[s, h], sem_ds.at[s, h])

        await_bytes(DS.at[s, 1 - h], sem_ds.at[s, 1 - h])

        @pl.when(r == 0)
        def _():
            await_bytes(T.at[pl.ds(0, 8 * (n_peer - 1)), :], sem_ds_s.at[s])

    def one_round(s):
        h0[...], l0[...] = load_pair(s, p)
        pair = (h0[...], l0[...])
        gram = dot3(pair, pair, NT)
        for n, (i, j) in enumerate(TILES):
            tile = gram[128 * i:128 * i + 128, 128 * j:128 * j + 128]
            if i == j:
                second = gram[128 * i + 128:128 * i + 256, 128 * i + 128:128 * i + 256]
                tile = jnp.where(column_ids >= row_ids, tile, second)
                D[s, i // 2:i // 2 + 1, :] = jnp.sum(jnp.where(on, second, 0.0), axis=0, keepdims=True)
            E[s, pl.ds(128 * n, 128), :] = tile

        own_at = (16 * x + 4 * z + y, 16 * y + 4 * z + x, 16 * z + 4 * x + y)
        line_at = (x, y, z)

        def piece_of(colour, k):
            first = part * k + sum(PIECES[:colour])
            return E.at[s, pl.ds(pl.multiple_of(first, 8), PIECES[colour]), :]

        send_diagonal(s)
        for colour, size in ORDER:
            def reduce_send(k, c2):
                k = lax.rem(21 * k, n_row)
                pr = 16 * lax.rem(zl + k // 16, 2) + 4 * lax.rem(x + k // 4, 4) + lax.rem(y + k, 4)
                pltpu.make_async_remote_copy(
                    src_ref=piece_of(colour, pr), dst_ref=RSB[colour].at[s, chunk(r, size), :],
                    send_sem=sem_rs_s.at[s, colour], recv_sem=sem_rs.at[s, colour],
                    device_id=(pr, p), device_id_type=MESH).start()
                return c2

            pltpu.make_async_copy(
                piece_of(colour, r), RSB[colour].at[s, chunk(r, size), :], sem_rs.at[s, colour]).start()
            lax.fori_loop(1, n_row, reduce_send, 0)

        for colour, size in ORDER:
            await_bytes(RSB[colour].at[s], sem_rs.at[s, colour])
            total = jnp.zeros((size, 128), F32)
            for k in range(n_row):
                total = total + RSB[colour][s, pl.ds(size * k, size), :]
            G[colour][s, chunk(own_at[colour], size), :] = total

            def plane_send(k, c2):
                k = lax.rem(7 * k, 16)
                near, far = lax.rem(k, 4), k // 4
                target = (device(0, near, far), device(near, 0, far), device(far, near, 0))[colour]
                piece = G[colour].at[s, chunk(own_at[colour], size), :]
                pltpu.make_async_remote_copy(
                    src_ref=piece, dst_ref=piece,
                    send_sem=sem_ag_s.at[s, colour, 0], recv_sem=sem_ag.at[s, colour, 0],
                    device_id=target, device_id_type=MESH).start()
                return c2

            lax.fori_loop(1, 16, plane_send, 0)
        sum_diagonal(s)
        for colour, size in ORDER:
            await_bytes(G[colour].at[s, pl.ds(0, 15 * size), :], sem_ag.at[s, colour, 0])
            line = G[colour].at[s, chunk(line_at[colour], 16 * size), :]
            for k in (2, 1, 3):
                pltpu.make_async_remote_copy(
                    src_ref=line, dst_ref=line,
                    send_sem=sem_ag_s.at[s, colour, 1], recv_sem=sem_ag.at[s, colour, 1],
                    device_id=(device(k, 0, 0), device(0, k, 0), device(0, 0, k))[colour],
                    device_id_type=MESH).start()
        for colour, size in ORDER:
            await_bytes(G[colour].at[s, pl.ds(0, 48 * size), :], sem_ag.at[s, colour, 1])
        await_diagonal(s)

        def rotate(hq, c2):
            for k in range(n_row):
                kz, kx, ky = 2 * hq + k // 16, (k // 4) % 4, k % 4
                first = part * k
                for colour, size in enumerate(PIECES):
                    at = (16 * kx + 4 * kz + ky, 16 * ky + 4 * kz + kx, 16 * kz + 4 * kx + ky)[colour]
                    T[pl.ds(first, size), :] = G[colour][s, chunk(at, size), :]
                    first += size
            tile = {ij: T[pl.ds(128 * n, 128), :] for n, ij in enumerate(TILES)}
            columns, rows = [], []
            for i in range(4):
                if i % 2 == 0:
                    diagonal = jnp.where(on, tile[i, i], 0.0)
                else:
                    diagonal = jnp.where(on, DS[s, hq, i // 2:i // 2 + 1, :], 0.0)
                columns.append(lax.rsqrt(jnp.sum(diagonal, axis=1, keepdims=True)))
                rows.append(lax.rsqrt(jnp.sum(diagonal, axis=0, keepdims=True)))
            squares = jnp.zeros((128, 128), F32)
            skew = {}
            for i, j in TILES:
                normed = tile[i, j] * columns[i] * rows[j]
                if i == j:
                    normed = jnp.where(column_ids > row_ids, normed, 0.0)
                    other = tile[i, i] * columns[i + 1] * rows[i + 1]
                    skew[i + 1, i + 1] = jnp.where(column_ids < row_ids, -other, 0.0)
                    squares = squares + skew[i + 1, i + 1] * skew[i + 1, i + 1]
                skew[i, j] = normed
                squares = squares + normed * normed
            scale = 1.0 / (1.0 + jnp.sqrt(2.0 * jnp.sum(squares, keepdims=True)))
            for i, j in skew:
                scaled = skew[i, j] * scale
                if i == j:
                    f0[pl.ds(128 * i, 128), pl.ds(128 * i, 128)] = scaled - scaled.T
                else:
                    f0[pl.ds(128 * i, 128), pl.ds(128 * j, 128)] = scaled
                    f0[pl.ds(128 * j, 128), pl.ds(128 * i, 128)] = -scaled.T
            h0[...], l0[...] = split(f0[...])
            square = dot(h0[...], h0[...])
            h1[...] = square.astype(BF16)
            f1[...] = (32.0 / 49.0) * square - (48.0 / 49.0) * f0[...] + jnp.where(eye, 48.0 / 49.0, 0.0)
            h2[...] = (f1[...] - (32.0 / 49.0) * dot(h0[...], h1[...])).astype(BF16)
            f0[...] = (
                jnp.where(eye, 1.0, 0.0) - h2[...].astype(F32) - (dot(h0[...], h2[...]) + dot(l0[...], h2[...])))
            h1[...] = f0[...].astype(BF16)
            square = dot(h1[...], h1[...])
            h3[...] = square.astype(BF16)
            h0[...], l0[...] = split(f0[...] + square)
            f0[...] = h2[...].astype(F32) + (dot(h2[...], h0[...]) + dot(h2[...], l0[...]))
            h2[...] = dot(h1[...], h3[...]).astype(BF16)
            h0[...] = f0[...].astype(BF16)
            inverse = f0[...] + dot(h0[...], h2[...])
            h0[...], l0[...] = split(2.0 * inverse - jnp.where(eye, 1.0, 0.0))
            q = 2 * hq + c
            h1[...], l1[...] = load_pair(s, q)
            turned = dot3((h0[...], l0[...]), (h1[...], l1[...]))
            for side in range(2):
                S[s + 1][2 * q + side] = turned[half * side:half * side + half]
            swap(s + 1, hq).start()
            return c2

        lax.fori_loop(0, 2, rotate, 0)
        for colour, size in ORDER:
            await_bytes(RSB[colour].at[s, pl.ds(0, size * (n_row - 1)), :], sem_rs_s.at[s, colour])
            await_bytes(G[colour].at[s, pl.ds(0, 15 * size), :], sem_ag_s.at[s, colour, 0])
            await_bytes(G[colour].at[s, pl.ds(0, 48 * size), :], sem_ag_s.at[s, colour, 1])
        await_swap(s + 1)

    one_round(0)
    one_round(1)
    for side in range(2):
        out[pl.ds(half * side, half), :] = S2[place(1, 2 * p + side)]


def deliver(blocks, out, sem):
    copy = pltpu.make_async_copy(blocks, out.at[:, 0, :], sem)
    copy.start()
    copy.wait()


def on_device(n_row, snapshots, plan):
    width = snapshots.shape[2] // n_row
    dma = pltpu.SemaphoreType.DMA
    full = (512, 512)
    result = pl.pallas_call(
        functools.partial(kernel, n_row),
        out_shape=jax.ShapeDtypeStruct((512, width), F32),
        in_specs=[pl.BlockSpec(memory_space=pltpu.SMEM), pl.BlockSpec(memory_space=pltpu.HBM)],
        out_specs=pl.BlockSpec(memory_space=pltpu.VMEM),
        scratch_shapes=[
            pltpu.VMEM((8, 256, width), F32), pltpu.VMEM((8, 256, width), F32), pltpu.VMEM((8, 256, width), F32),
            pltpu.VMEM((2, TILE_ROWS, 128), F32),
            *[pltpu.VMEM((2, n_row * size, 128), F32) for size in PIECES],
            *[pltpu.VMEM((2, 64 * size, 128), F32) for size in PIECES],
            pltpu.VMEM((TILE_ROWS, 128), F32),
            pltpu.VMEM((2, 8, 128), F32), pltpu.VMEM((2, n_row, 8, 128), F32), pltpu.VMEM((2, 2, 8, 128), F32),
            pltpu.VMEM(full, F32), pltpu.VMEM(full, F32),
            pltpu.VMEM(full, BF16), pltpu.VMEM(full, BF16), pltpu.VMEM(full, BF16), pltpu.VMEM(full, BF16),
            pltpu.VMEM(full, BF16), pltpu.VMEM(full, BF16),
            dma((2,)), dma((2,)), dma((2, 2)), dma((2,)), dma((2 * n_row,)), dma, dma, dma, dma((2, 2)), dma((2, 2)), dma((2, 3)), dma((2, 3)), dma((2, 3, 2)), dma((2, 3, 2)),
        ],
        compiler_params=pltpu.CompilerParams(
            collective_id=0, has_side_effects=True, vmem_limit_bytes=32 * 1024 * 1024),
    )(pltpu.with_memory_space_constraint(plan, pltpu.HBM), pltpu.with_memory_space_constraint(snapshots, pltpu.HBM))
    return pl.pallas_call(
        deliver,
        out_shape=jax.ShapeDtypeStruct((512, 1, width), F32),
        in_specs=[pl.BlockSpec(memory_space=pl.ANY)],
        out_specs=pl.BlockSpec(memory_space=pltpu.HBM),
        scratch_shapes=[dma],
        compiler_params=pltpu.CompilerParams(vmem_limit_bytes=4 * 1024 * 1024),
    )(result)


def solution(mesh):
    n_row = mesh.shape["row"]
    return jax.shard_map(
        functools.partial(on_device, n_row), mesh=mesh,
        in_specs=(P("row", "pair", None), P()), out_specs=P(None, "pair", "row"), check_vma=False)
```

```python
import functools

import jax
import jax.numpy as jnp
from jax import lax
from jax.experimental import pallas as pl
from jax.experimental.pallas import tpu as pltpu
from jax.sharding import PartitionSpec as P

MESH = pl.DeviceIdType.MESH
F32 = jnp.float32
BF16 = jnp.bfloat16
NN = (((1,), (0,)), ((), ()))
NT = (((1,), (1,)), ((), ()))
TILES = [(i, j) for i in range(4) for j in range(i + 1, 4)] + [(0, 0), (2, 2)]
TILE_ROWS = 128 * len(TILES)
PIECES = (8, 8, 16)
ORDER = [(2, PIECES[2]), (0, PIECES[0]), (1, PIECES[1])]


def dot(left, right, dims=NN):
    return lax.dot_general(left, right, dims, preferred_element_type=F32)


def chunk(at, size):
    return pl.ds(pl.multiple_of(size * at, size), size)


def split(value):
    high = value.astype(BF16)
    return high, (value - high.astype(F32)).astype(BF16)


def dot3(left, right, dims=NN):
    (left_high, left_low), (right_high, right_low) = left, right
    return (
        dot(left_high, right_high, dims)
        + dot(left_high, right_low, dims)
        + dot(left_low, right_high, dims)
    )


def identity(size):
    shape = (size, size)
    return lax.broadcasted_iota(jnp.int32, shape, 0) == lax.broadcasted_iota(jnp.int32, shape, 1)


def kernel(n_row, plan, snap, out, S0, S1, S2, E, B0, B1, B2, G0, G1, G2, T, D, DB, DS, f0, f1, h0, l0, h1, l1, h2, h3,
           sem_d, sem_d_s, sem_ds, sem_ds_s, sem_in, sem_in_s, sem_fw, sem_fw_s, sem_sw, sem_sw_s, sem_rs, sem_rs_s, sem_ag, sem_ag_s):
    r = lax.axis_index("row")
    p = lax.axis_index("pair")
    h, c = p // 2, p % 2
    n_peer = 2 * n_row
    me = h * n_row + r
    part = TILE_ROWS // n_row
    order = 512
    half = 256
    S = (S0, S1, S2)
    G = (G0, G1, G2)
    RSB = (B0, B1, B2)
    width = S0.shape[2]
    own = snap.shape[0]
    partner = (r, 2 * h + 1 - c)

    zl, x, y = r // 16, lax.rem(r // 4, 4), lax.rem(r, 4)
    z = 2 * h + zl

    def device(dx, dy, dz):
        px, py, pz = lax.rem(x + dx, 4), lax.rem(y + dy, 4), lax.rem(z + dz, 4)
        return 16 * lax.rem(pz, 2) + 4 * px + py, 2 * (pz // 2) + c

    def peer_of(k):
        k = lax.rem(37 * k, n_peer)
        return device(lax.rem(k // 4, 4), lax.rem(k, 4), k // 16)

    def source_of(k):
        k = lax.rem(37 * k, n_peer)
        return device(lax.rem(4 - k // 4 % 4, 4), lax.rem(4 - k % 4, 4), lax.rem(4 - k // 16, 4))

    barrier = pltpu.get_barrier_semaphore()

    def greet(k, carry):
        pl.semaphore_signal(barrier, inc=1, device_id=peer_of(k), device_id_type=MESH)
        return carry

    pl.semaphore_signal(barrier, inc=1, device_id=partner, device_id_type=MESH)
    lax.fori_loop(1, n_peer, greet, 0)
    pl.semaphore_wait(barrier, n_peer)

    def home(row_at, pair_at):
        first = own * row_at
        return S0.at[2 * pair_at + first // half, pl.ds(pl.multiple_of(lax.rem(first, half), own), own), :]

    def columns_for(row_at):
        return snap.at[:, 0, pl.ds(pl.multiple_of(width * row_at, width), width)]

    local = pltpu.make_async_copy(columns_for(r), home(r, p), sem_in.at[0])
    local.start()

    def scatter(k, carry):
        pr, pp = peer_of(k)
        pltpu.make_async_remote_copy(
            src_ref=columns_for(pr), dst_ref=home(r, p),
            send_sem=sem_in_s, recv_sem=sem_in.at[k],
            device_id=(pr, pp), device_id_type=MESH).start()
        return carry

    lax.fori_loop(1, n_peer, scatter, 0)

    def forward(k, carry):
        arrived = home(*source_of(k))
        await_bytes(arrived, sem_in.at[k])
        pltpu.make_async_remote_copy(
            src_ref=arrived, dst_ref=arrived, send_sem=sem_fw_s, recv_sem=sem_fw,
            device_id=partner, device_id_type=MESH).start()
        return carry

    def await_bytes(ref, sem):
        pltpu.make_async_copy(ref, ref, sem).wait()

    lax.fori_loop(0, n_peer, forward, 0)
    await_bytes(S0.at[pl.ds(0, 6), pl.ds(0, own * (n_peer - 1) // 6), :], sem_in_s)
    await_bytes(S0.at[pl.ds(0, 4)], sem_fw)
    await_bytes(S0.at[pl.ds(0, 4)], sem_fw_s)

    def swap(s, hq, side):
        block = S[s].at[2 * (2 * hq + c) + side]
        return pltpu.make_async_remote_copy(
            src_ref=block, dst_ref=block,
            send_sem=sem_sw_s.at[s - 1, hq, side], recv_sem=sem_sw.at[s - 1, hq, side],
            device_id=partner, device_id_type=MESH)

    def await_swap(s):
        for hq in range(2):
            for side in range(2):
                other = S[s].at[2 * (2 * hq + 1 - c) + side]
                await_bytes(other, sem_sw.at[s - 1, hq, side])
                await_bytes(other, sem_sw_s.at[s - 1, hq, side])

    eye = identity(order)
    on = identity(128)
    row_ids = lax.broadcasted_iota(jnp.int32, (128, 128), 0)
    column_ids = lax.broadcasted_iota(jnp.int32, (128, 128), 1)
    D[...] = jnp.zeros_like(D)

    def place(round_at, block):
        at = jnp.int32(0)
        for k in range(1, 8):
            at = at + k * (plan[round_at, k] == block).astype(jnp.int32)
        return jnp.minimum(at, 7)

    def load_pair(s, q):
        wanted = [plan[s, 2 * q + side] for side in range(2)]
        parts = [S[s][block if s == 0 else place(0, block)] for block in wanted]
        return split(jnp.concatenate(parts, axis=0))

    def send_diagonal(s):
        @pl.when(r > 0)
        def _():
            pltpu.make_async_remote_copy(
                src_ref=D.at[s], dst_ref=DB.at[s, r], send_sem=sem_d_s.at[s], recv_sem=sem_d.at[s],
                device_id=(0, p), device_id_type=MESH).start()

    def sum_diagonal(s):
        @pl.when(r == 0)
        def _():
            await_bytes(DB.at[s, pl.ds(1, n_row - 1)], sem_d.at[s])
            total = D[s]
            for k in range(1, n_row):
                total = total + DB[s, k]
            DS[s, h] = total

            def send(k, carry):
                pltpu.make_async_remote_copy(
                    src_ref=DS.at[s, h], dst_ref=DS.at[s, h], send_sem=sem_ds_s.at[s], recv_sem=sem_ds.at[s, h],
                    device_id=peer_of(k), device_id_type=MESH).start()
                return carry

            lax.fori_loop(1, n_peer, send, 0)

    def await_diagonal(s):
        @pl.when(r > 0)
        def _():
            await_bytes(D.at[s], sem_d_s.at[s])
            await_bytes(DS.at[s, h], sem_ds.at[s, h])

        await_bytes(DS.at[s, 1 - h], sem_ds.at[s, 1 - h])

        @pl.when(r == 0)
        def _():
            await_bytes(T.at[pl.ds(0, 8 * (n_peer - 1)), :], sem_ds_s.at[s])

    def one_round(s):
        h0[...], l0[...] = load_pair(s, p)
        pair = (h0[...], l0[...])
        upper = dot3((h0[:half], l0[:half]), pair, NT)
        lower = dot3((h0[half:], l0[half:]), (h0[half:], l0[half:]), NT)

        def gram_tile(i, j):
            at = 128 * i if i < 2 else 128 * i - half
            source, shift = (upper, 0) if i < 2 else (lower, half)
            return source[at:at + 128, 128 * j - shift:128 * j - shift + 128]

        for n, (i, j) in enumerate(TILES):
            tile = gram_tile(i, j)
            if i == j:
                second = gram_tile(i + 1, i + 1)
                tile = jnp.where(column_ids >= row_ids, tile, second)
                D[s, i // 2:i // 2 + 1, :] = jnp.sum(jnp.where(on, second, 0.0), axis=0, keepdims=True)
            E[s, pl.ds(128 * n, 128), :] = tile

        own_at = (16 * x + 4 * z + y, 16 * y + 4 * z + x, 16 * z + 4 * x + y)
        line_at = (x, y, z)

        def piece_of(colour, k):
            first = part * k + sum(PIECES[:colour])
            return E.at[s, pl.ds(pl.multiple_of(first, 8), PIECES[colour]), :]

        send_diagonal(s)
        for colour, size in ORDER:
            def reduce_send(k, c2):
                k = lax.rem(21 * k, n_row)
                pr = 16 * lax.rem(zl + k // 16, 2) + 4 * lax.rem(x + k // 4, 4) + lax.rem(y + k, 4)
                pltpu.make_async_remote_copy(
                    src_ref=piece_of(colour, pr), dst_ref=RSB[colour].at[s, chunk(r, size), :],
                    send_sem=sem_rs_s.at[s, colour], recv_sem=sem_rs.at[s, colour],
                    device_id=(pr, p), device_id_type=MESH).start()
                return c2

            pltpu.make_async_copy(
                piece_of(colour, r), RSB[colour].at[s, chunk(r, size), :], sem_rs.at[s, colour]).start()
            lax.fori_loop(1, n_row, reduce_send, 0)

        for colour, size in ORDER:
            await_bytes(RSB[colour].at[s], sem_rs.at[s, colour])
            total = jnp.zeros((size, 128), F32)
            for k in range(n_row):
                total = total + RSB[colour][s, pl.ds(size * k, size), :]
            G[colour][s, chunk(own_at[colour], size), :] = total

            def plane_send(k, c2):
                k = lax.rem(7 * k, 16)
                near, far = lax.rem(k, 4), k // 4
                target = (device(0, near, far), device(near, 0, far), device(far, near, 0))[colour]
                piece = G[colour].at[s, chunk(own_at[colour], size), :]
                pltpu.make_async_remote_copy(
                    src_ref=piece, dst_ref=piece,
                    send_sem=sem_ag_s.at[s, colour, 0], recv_sem=sem_ag.at[s, colour, 0],
                    device_id=target, device_id_type=MESH).start()
                return c2

            lax.fori_loop(1, 16, plane_send, 0)
        sum_diagonal(s)
        for colour, size in ORDER:
            await_bytes(G[colour].at[s, pl.ds(0, 15 * size), :], sem_ag.at[s, colour, 0])
            line = G[colour].at[s, chunk(line_at[colour], 16 * size), :]
            for k in (2, 1, 3):
                pltpu.make_async_remote_copy(
                    src_ref=line, dst_ref=line,
                    send_sem=sem_ag_s.at[s, colour, 1], recv_sem=sem_ag.at[s, colour, 1],
                    device_id=(device(k, 0, 0), device(0, k, 0), device(0, 0, k))[colour],
                    device_id_type=MESH).start()
        for colour, size in ORDER:
            await_bytes(G[colour].at[s, pl.ds(0, 48 * size), :], sem_ag.at[s, colour, 1])
        await_diagonal(s)

        def rotate(hq, c2):
            for k in range(n_row):
                kz, kx, ky = 2 * hq + k // 16, (k // 4) % 4, k % 4
                first = part * k
                for colour, size in enumerate(PIECES):
                    at = (16 * kx + 4 * kz + ky, 16 * ky + 4 * kz + kx, 16 * kz + 4 * kx + ky)[colour]
                    T[pl.ds(first, size), :] = G[colour][s, chunk(at, size), :]
                    first += size
            tile = {ij: T[pl.ds(128 * n, 128), :] for n, ij in enumerate(TILES)}
            columns, rows = [], []
            for i in range(4):
                if i % 2 == 0:
                    diagonal = jnp.where(on, tile[i, i], 0.0)
                else:
                    diagonal = jnp.where(on, DS[s, hq, i // 2:i // 2 + 1, :], 0.0)
                columns.append(lax.rsqrt(jnp.sum(diagonal, axis=1, keepdims=True)))
                rows.append(lax.rsqrt(jnp.sum(diagonal, axis=0, keepdims=True)))
            squares = jnp.zeros((128, 128), F32)
            skew = {}
            for i, j in TILES:
                normed = tile[i, j] * columns[i] * rows[j]
                if i == j:
                    normed = jnp.where(column_ids > row_ids, normed, 0.0)
                    other = tile[i, i] * columns[i + 1] * rows[i + 1]
                    skew[i + 1, i + 1] = jnp.where(column_ids < row_ids, -other, 0.0)
                    squares = squares + skew[i + 1, i + 1] * skew[i + 1, i + 1]
                skew[i, j] = normed
                squares = squares + normed * normed
            scale = 1.0 / (1.0 + jnp.sqrt(2.0 * jnp.sum(squares, keepdims=True)))
            for i, j in skew:
                scaled = skew[i, j] * scale
                if i == j:
                    f0[pl.ds(128 * i, 128), pl.ds(128 * i, 128)] = scaled - scaled.T
                else:
                    f0[pl.ds(128 * i, 128), pl.ds(128 * j, 128)] = scaled
                    f0[pl.ds(128 * j, 128), pl.ds(128 * i, 128)] = -scaled.T
            h0[...], l0[...] = split(f0[...])
            square = dot(h0[...], h0[...])
            h1[...] = square.astype(BF16)
            f1[...] = (32.0 / 49.0) * square - (48.0 / 49.0) * f0[...] + jnp.where(eye, 48.0 / 49.0, 0.0)
            h2[...] = (f1[...] - (32.0 / 49.0) * dot(h0[...], h1[...])).astype(BF16)
            f0[...] = (
                jnp.where(eye, 1.0, 0.0) - h2[...].astype(F32) - (dot(h0[...], h2[...]) + dot(l0[...], h2[...])))
            h1[...] = f0[...].astype(BF16)
            square = dot(h1[...], h1[...])
            h3[...] = square.astype(BF16)
            h0[...], l0[...] = split(f0[...] + square)
            f0[...] = h2[...].astype(F32) + (dot(h2[...], h0[...]) + dot(h2[...], l0[...]))
            h2[...] = dot(h1[...], h3[...]).astype(BF16)
            h0[...] = f0[...].astype(BF16)
            inverse = f0[...] + dot(h0[...], h2[...])
            h0[...], l0[...] = split(2.0 * inverse - jnp.where(eye, 1.0, 0.0))
            q = 2 * hq + c
            h1[...], l1[...] = load_pair(s, q)
            for side in range(2):
                part_of = pl.ds(half * side, half)
                S[s + 1][2 * q + side] = dot3((h0[part_of, :], l0[part_of, :]), (h1[...], l1[...]))
                swap(s + 1, hq, side).start()
            return c2

        lax.fori_loop(0, 2, rotate, 0)
        for colour, size in ORDER:
            await_bytes(RSB[colour].at[s, pl.ds(0, size * (n_row - 1)), :], sem_rs_s.at[s, colour])
            await_bytes(G[colour].at[s, pl.ds(0, 15 * size), :], sem_ag_s.at[s, colour, 0])
            await_bytes(G[colour].at[s, pl.ds(0, 48 * size), :], sem_ag_s.at[s, colour, 1])
        await_swap(s + 1)

    one_round(0)
    one_round(1)
    for side in range(2):
        out[pl.ds(half * side, half), :] = S2[place(1, 2 * p + side)]


def deliver(blocks, out, sem):
    copy = pltpu.make_async_copy(blocks, out.at[:, 0, :], sem)
    copy.start()
    copy.wait()


def on_device(n_row, snapshots, plan):
    width = snapshots.shape[2] // n_row
    dma = pltpu.SemaphoreType.DMA
    full = (512, 512)
    result = pl.pallas_call(
        functools.partial(kernel, n_row),
        out_shape=jax.ShapeDtypeStruct((512, width), F32),
        in_specs=[pl.BlockSpec(memory_space=pltpu.SMEM), pl.BlockSpec(memory_space=pltpu.HBM)],
        out_specs=pl.BlockSpec(memory_space=pltpu.VMEM),
        scratch_shapes=[
            pltpu.VMEM((8, 256, width), F32), pltpu.VMEM((8, 256, width), F32), pltpu.VMEM((8, 256, width), F32),
            pltpu.VMEM((2, TILE_ROWS, 128), F32),
            *[pltpu.VMEM((2, n_row * size, 128), F32) for size in PIECES],
            *[pltpu.VMEM((2, 64 * size, 128), F32) for size in PIECES],
            pltpu.VMEM((TILE_ROWS, 128), F32),
            pltpu.VMEM((2, 8, 128), F32), pltpu.VMEM((2, n_row, 8, 128), F32), pltpu.VMEM((2, 2, 8, 128), F32),
            pltpu.VMEM(full, F32), pltpu.VMEM(full, F32),
            pltpu.VMEM(full, BF16), pltpu.VMEM(full, BF16), pltpu.VMEM(full, BF16), pltpu.VMEM(full, BF16),
            pltpu.VMEM(full, BF16), pltpu.VMEM(full, BF16),
            dma((2,)), dma((2,)), dma((2, 2)), dma((2,)), dma((2 * n_row,)), dma, dma, dma, dma((2, 2, 2)), dma((2, 2, 2)), dma((2, 3)), dma((2, 3)), dma((2, 3, 2)), dma((2, 3, 2)),
        ],
        compiler_params=pltpu.CompilerParams(
            collective_id=0, has_side_effects=True, vmem_limit_bytes=32 * 1024 * 1024),
    )(pltpu.with_memory_space_constraint(plan, pltpu.HBM), pltpu.with_memory_space_constraint(snapshots, pltpu.HBM))
    return pl.pallas_call(
        deliver,
        out_shape=jax.ShapeDtypeStruct((512, 1, width), F32),
        in_specs=[pl.BlockSpec(memory_space=pl.ANY)],
        out_specs=pl.BlockSpec(memory_space=pltpu.HBM),
        scratch_shapes=[dma],
        compiler_params=pltpu.CompilerParams(vmem_limit_bytes=4 * 1024 * 1024),
    )(result)


def solution(mesh):
    n_row = mesh.shape["row"]
    return jax.shard_map(
        functools.partial(on_device, n_row), mesh=mesh,
        in_specs=(P("row", "pair", None), P()), out_specs=P(None, "pair", "row"), check_vma=False)
```

```python
import functools

import jax
import jax.numpy as jnp
from jax import lax
from jax.experimental import pallas as pl
from jax.experimental.pallas import tpu as pltpu
from jax.sharding import PartitionSpec as P

MESH = pl.DeviceIdType.MESH
F32 = jnp.float32
BF16 = jnp.bfloat16
NN = (((1,), (0,)), ((), ()))
NT = (((1,), (1,)), ((), ()))
TILES = [(i, j) for i in range(4) for j in range(i + 1, 4)] + [(0, 0), (2, 2)]
TILE_ROWS = 128 * len(TILES)
PIECES = (8, 8, 16)
ORDER = [(2, PIECES[2]), (1, PIECES[1]), (0, PIECES[0])]


def dot(left, right, dims=NN):
    return lax.dot_general(left, right, dims, preferred_element_type=F32)


def chunk(at, size):
    return pl.ds(pl.multiple_of(size * at, size), size)


def split(value):
    high = value.astype(BF16)
    return high, (value - high.astype(F32)).astype(BF16)


def dot3(left, right, dims=NN):
    (left_high, left_low), (right_high, right_low) = left, right
    return (
        dot(left_high, right_high, dims)
        + dot(left_high, right_low, dims)
        + dot(left_low, right_high, dims)
    )


def identity(size):
    shape = (size, size)
    return lax.broadcasted_iota(jnp.int32, shape, 0) == lax.broadcasted_iota(jnp.int32, shape, 1)


def kernel(n_row, plan, snap, out, S0, S1, S2, E, B0, B1, B2, G0, G1, G2, T, D, DB, DS, f0, f1, h0, l0, h1, l1, h2, h3,
           sem_d, sem_d_s, sem_ds, sem_ds_s, sem_in, sem_in_s, sem_fw, sem_fw_s, sem_sw, sem_sw_s, sem_rs, sem_rs_s, sem_ag, sem_ag_s):
    r = lax.axis_index("row")
    p = lax.axis_index("pair")
    h, c = p // 2, p % 2
    n_peer = 2 * n_row
    me = h * n_row + r
    part = TILE_ROWS // n_row
    order = 512
    half = 256
    S = (S0, S1, S2)
    G = (G0, G1, G2)
    RSB = (B0, B1, B2)
    width = S0.shape[2]
    own = snap.shape[0]
    partner = (r, 2 * h + 1 - c)

    zl, x, y = r // 16, lax.rem(r // 4, 4), lax.rem(r, 4)
    z = 2 * h + zl

    def device(dx, dy, dz):
        px, py, pz = lax.rem(x + dx, 4), lax.rem(y + dy, 4), lax.rem(z + dz, 4)
        return 16 * lax.rem(pz, 2) + 4 * px + py, 2 * (pz // 2) + c

    def peer_of(k):
        k = lax.rem(37 * k, n_peer)
        return device(lax.rem(k // 4, 4), lax.rem(k, 4), k // 16)

    def source_of(k):
        k = lax.rem(37 * k, n_peer)
        return device(lax.rem(4 - k // 4 % 4, 4), lax.rem(4 - k % 4, 4), lax.rem(4 - k // 16, 4))

    barrier = pltpu.get_barrier_semaphore()

    def greet(k, carry):
        pl.semaphore_signal(barrier, inc=1, device_id=peer_of(k), device_id_type=MESH)
        return carry

    pl.semaphore_signal(barrier, inc=1, device_id=partner, device_id_type=MESH)
    lax.fori_loop(1, n_peer, greet, 0)
    pl.semaphore_wait(barrier, n_peer)

    def home(row_at, pair_at):
        first = own * row_at
        return S0.at[2 * pair_at + first // half, pl.ds(pl.multiple_of(lax.rem(first, half), own), own), :]

    def columns_for(row_at):
        return snap.at[:, 0, pl.ds(pl.multiple_of(width * row_at, width), width)]

    local = pltpu.make_async_copy(columns_for(r), home(r, p), sem_in.at[0])
    local.start()

    def scatter(k, carry):
        pr, pp = peer_of(k)
        pltpu.make_async_remote_copy(
            src_ref=columns_for(pr), dst_ref=home(r, p),
            send_sem=sem_in_s, recv_sem=sem_in.at[k],
            device_id=(pr, pp), device_id_type=MESH).start()
        return carry

    lax.fori_loop(1, n_peer, scatter, 0)

    def forward(k, carry):
        arrived = home(*source_of(k))
        await_bytes(arrived, sem_in.at[k])
        pltpu.make_async_remote_copy(
            src_ref=arrived, dst_ref=arrived, send_sem=sem_fw_s, recv_sem=sem_fw,
            device_id=partner, device_id_type=MESH).start()
        return carry

    def await_bytes(ref, sem):
        pltpu.make_async_copy(ref, ref, sem).wait()

    lax.fori_loop(0, n_peer, forward, 0)
    await_bytes(S0.at[pl.ds(0, 6), pl.ds(0, own * (n_peer - 1) // 6), :], sem_in_s)
    await_bytes(S0.at[pl.ds(0, 4)], sem_fw)
    await_bytes(S0.at[pl.ds(0, 4)], sem_fw_s)

    def swap(s, hq, side):
        block = S[s].at[2 * (2 * hq + c) + side]
        return pltpu.make_async_remote_copy(
            src_ref=block, dst_ref=block,
            send_sem=sem_sw_s.at[s - 1, hq, side], recv_sem=sem_sw.at[s - 1, hq, side],
            device_id=partner, device_id_type=MESH)

    def await_swap(s):
        for hq in range(2):
            for side in range(2):
                other = S[s].at[2 * (2 * hq + 1 - c) + side]
                await_bytes(other, sem_sw.at[s - 1, hq, side])
                await_bytes(other, sem_sw_s.at[s - 1, hq, side])

    eye = identity(order)
    on = identity(128)
    row_ids = lax.broadcasted_iota(jnp.int32, (128, 128), 0)
    column_ids = lax.broadcasted_iota(jnp.int32, (128, 128), 1)
    D[...] = jnp.zeros_like(D)

    def place(round_at, block):
        at = jnp.int32(0)
        for k in range(1, 8):
            at = at + k * (plan[round_at, k] == block).astype(jnp.int32)
        return jnp.minimum(at, 7)

    def load_pair(s, q):
        wanted = [plan[s, 2 * q + side] for side in range(2)]
        parts = [S[s][block if s == 0 else place(0, block)] for block in wanted]
        return split(jnp.concatenate(parts, axis=0))

    def send_diagonal(s):
        @pl.when(r > 0)
        def _():
            pltpu.make_async_remote_copy(
                src_ref=D.at[s], dst_ref=DB.at[s, r], send_sem=sem_d_s.at[s], recv_sem=sem_d.at[s],
                device_id=(0, p), device_id_type=MESH).start()

    def sum_diagonal(s):
        @pl.when(r == 0)
        def _():
            await_bytes(DB.at[s, pl.ds(1, n_row - 1)], sem_d.at[s])
            total = D[s]
            for k in range(1, n_row):
                total = total + DB[s, k]
            DS[s, h] = total

            def send(k, carry):
                pltpu.make_async_remote_copy(
                    src_ref=DS.at[s, h], dst_ref=DS.at[s, h], send_sem=sem_ds_s.at[s], recv_sem=sem_ds.at[s, h],
                    device_id=peer_of(k), device_id_type=MESH).start()
                return carry

            lax.fori_loop(1, n_peer, send, 0)

    def await_diagonal(s):
        @pl.when(r > 0)
        def _():
            await_bytes(D.at[s], sem_d_s.at[s])
            await_bytes(DS.at[s, h], sem_ds.at[s, h])

        await_bytes(DS.at[s, 1 - h], sem_ds.at[s, 1 - h])

        @pl.when(r == 0)
        def _():
            await_bytes(T.at[pl.ds(0, 8 * (n_peer - 1)), :], sem_ds_s.at[s])

    def one_round(s):
        h0[...], l0[...] = load_pair(s, p)
        pair = (h0[...], l0[...])
        upper = dot3((h0[:half], l0[:half]), pair, NT)
        lower = dot3((h0[half:], l0[half:]), (h0[half:], l0[half:]), NT)

        def gram_tile(i, j):
            at = 128 * i if i < 2 else 128 * i - half
            source, shift = (upper, 0) if i < 2 else (lower, half)
            return source[at:at + 128, 128 * j - shift:128 * j - shift + 128]

        for n, (i, j) in enumerate(TILES):
            tile = gram_tile(i, j)
            if i == j:
                second = gram_tile(i + 1, i + 1)
                tile = jnp.where(column_ids >= row_ids, tile, second)
                D[s, i // 2:i // 2 + 1, :] = jnp.sum(jnp.where(on, second, 0.0), axis=0, keepdims=True)
            E[s, pl.ds(128 * n, 128), :] = tile

        own_at = (16 * x + 4 * z + y, 16 * y + 4 * z + x, 16 * z + 4 * x + y)
        line_at = (x, y, z)

        def piece_of(colour, k):
            first = part * k + sum(PIECES[:colour])
            return E.at[s, pl.ds(pl.multiple_of(first, 8), PIECES[colour]), :]

        send_diagonal(s)
        for colour, size in ORDER:
            def reduce_send(k, c2):
                k = lax.rem(21 * k, n_row)
                pr = 16 * lax.rem(zl + k // 16, 2) + 4 * lax.rem(x + k // 4, 4) + lax.rem(y + k, 4)
                pltpu.make_async_remote_copy(
                    src_ref=piece_of(colour, pr), dst_ref=RSB[colour].at[s, chunk(r, size), :],
                    send_sem=sem_rs_s.at[s, colour], recv_sem=sem_rs.at[s, colour],
                    device_id=(pr, p), device_id_type=MESH).start()
                return c2

            pltpu.make_async_copy(
                piece_of(colour, r), RSB[colour].at[s, chunk(r, size), :], sem_rs.at[s, colour]).start()
            lax.fori_loop(1, n_row, reduce_send, 0)

        for colour, size in ORDER:
            await_bytes(RSB[colour].at[s], sem_rs.at[s, colour])
            total = jnp.zeros((size, 128), F32)
            for k in range(n_row):
                total = total + RSB[colour][s, pl.ds(size * k, size), :]
            G[colour][s, chunk(own_at[colour], size), :] = total

            def plane_send(k, c2):
                k = lax.rem(7 * k, 16)
                near, far = lax.rem(k, 4), k // 4
                target = (device(0, near, far), device(near, 0, far), device(far, near, 0))[colour]
                piece = G[colour].at[s, chunk(own_at[colour], size), :]
                pltpu.make_async_remote_copy(
                    src_ref=piece, dst_ref=piece,
                    send_sem=sem_ag_s.at[s, colour, 0], recv_sem=sem_ag.at[s, colour, 0],
                    device_id=target, device_id_type=MESH).start()
                return c2

            lax.fori_loop(1, 16, plane_send, 0)
        sum_diagonal(s)
        for colour, size in ORDER:
            await_bytes(G[colour].at[s, pl.ds(0, 15 * size), :], sem_ag.at[s, colour, 0])
            line = G[colour].at[s, chunk(line_at[colour], 16 * size), :]
            for k in (2, 1, 3):
                pltpu.make_async_remote_copy(
                    src_ref=line, dst_ref=line,
                    send_sem=sem_ag_s.at[s, colour, 1], recv_sem=sem_ag.at[s, colour, 1],
                    device_id=(device(k, 0, 0), device(0, k, 0), device(0, 0, k))[colour],
                    device_id_type=MESH).start()
        for colour, size in ORDER:
            await_bytes(G[colour].at[s, pl.ds(0, 48 * size), :], sem_ag.at[s, colour, 1])
        await_diagonal(s)

        def rotate(hq, c2):
            for k in range(n_row):
                kz, kx, ky = 2 * hq + k // 16, (k // 4) % 4, k % 4
                first = part * k
                for colour, size in enumerate(PIECES):
                    at = (16 * kx + 4 * kz + ky, 16 * ky + 4 * kz + kx, 16 * kz + 4 * kx + ky)[colour]
                    T[pl.ds(first, size), :] = G[colour][s, chunk(at, size), :]
                    first += size
            tile = {ij: T[pl.ds(128 * n, 128), :] for n, ij in enumerate(TILES)}
            columns, rows = [], []
            for i in range(4):
                if i % 2 == 0:
                    diagonal = jnp.where(on, tile[i, i], 0.0)
                else:
                    diagonal = jnp.where(on, DS[s, hq, i // 2:i // 2 + 1, :], 0.0)
                columns.append(lax.rsqrt(jnp.sum(diagonal, axis=1, keepdims=True)))
                rows.append(lax.rsqrt(jnp.sum(diagonal, axis=0, keepdims=True)))
            squares = jnp.zeros((128, 128), F32)
            skew = {}
            for i, j in TILES:
                normed = tile[i, j] * columns[i] * rows[j]
                if i == j:
                    normed = jnp.where(column_ids > row_ids, normed, 0.0)
                    other = tile[i, i] * columns[i + 1] * rows[i + 1]
                    skew[i + 1, i + 1] = jnp.where(column_ids < row_ids, -other, 0.0)
                    squares = squares + skew[i + 1, i + 1] * skew[i + 1, i + 1]
                skew[i, j] = normed
                squares = squares + normed * normed
            scale = 1.0 / (1.0 + jnp.sqrt(2.0 * jnp.sum(squares, keepdims=True)))
            for i, j in skew:
                scaled = skew[i, j] * scale
                if i == j:
                    f0[pl.ds(128 * i, 128), pl.ds(128 * i, 128)] = scaled - scaled.T
                else:
                    f0[pl.ds(128 * i, 128), pl.ds(128 * j, 128)] = scaled
                    f0[pl.ds(128 * j, 128), pl.ds(128 * i, 128)] = -scaled.T
            h0[...], l0[...] = split(f0[...])
            square = dot(h0[...], h0[...])
            h1[...] = square.astype(BF16)
            f1[...] = (32.0 / 49.0) * square - (48.0 / 49.0) * f0[...] + jnp.where(eye, 48.0 / 49.0, 0.0)
            h2[...] = (f1[...] - (32.0 / 49.0) * dot(h0[...], h1[...])).astype(BF16)
            f0[...] = (
                jnp.where(eye, 1.0, 0.0) - h2[...].astype(F32) - (dot(h0[...], h2[...]) + dot(l0[...], h2[...])))
            h1[...] = f0[...].astype(BF16)
            square = dot(h1[...], h1[...])
            h3[...] = square.astype(BF16)
            h0[...], l0[...] = split(f0[...] + square)
            f0[...] = h2[...].astype(F32) + (dot(h2[...], h0[...]) + dot(h2[...], l0[...]))
            h2[...] = dot(h1[...], h3[...]).astype(BF16)
            h0[...] = f0[...].astype(BF16)
            inverse = f0[...] + dot(h0[...], h2[...])
            h0[...], l0[...] = split(2.0 * inverse - jnp.where(eye, 1.0, 0.0))
            q = 2 * hq + c
            h1[...], l1[...] = load_pair(s, q)
            for side in range(2):
                part_of = pl.ds(half * side, half)
                S[s + 1][2 * q + side] = dot3((h0[part_of, :], l0[part_of, :]), (h1[...], l1[...]))
                swap(s + 1, hq, side).start()
            return c2

        lax.fori_loop(0, 2, rotate, 0)
        for colour, size in ORDER:
            await_bytes(RSB[colour].at[s, pl.ds(0, size * (n_row - 1)), :], sem_rs_s.at[s, colour])
            await_bytes(G[colour].at[s, pl.ds(0, 15 * size), :], sem_ag_s.at[s, colour, 0])
            await_bytes(G[colour].at[s, pl.ds(0, 48 * size), :], sem_ag_s.at[s, colour, 1])
        await_swap(s + 1)

    one_round(0)
    one_round(1)
    for side in range(2):
        out[pl.ds(half * side, half), :] = S2[place(1, 2 * p + side)]


def deliver(blocks, out, sem):
    copy = pltpu.make_async_copy(blocks, out.at[:, 0, :], sem)
    copy.start()
    copy.wait()


def on_device(n_row, snapshots, plan):
    width = snapshots.shape[2] // n_row
    dma = pltpu.SemaphoreType.DMA
    full = (512, 512)
    result = pl.pallas_call(
        functools.partial(kernel, n_row),
        out_shape=jax.ShapeDtypeStruct((512, width), F32),
        in_specs=[pl.BlockSpec(memory_space=pltpu.SMEM), pl.BlockSpec(memory_space=pltpu.HBM)],
        out_specs=pl.BlockSpec(memory_space=pltpu.VMEM),
        scratch_shapes=[
            pltpu.VMEM((8, 256, width), F32), pltpu.VMEM((8, 256, width), F32), pltpu.VMEM((8, 256, width), F32),
            pltpu.VMEM((2, TILE_ROWS, 128), F32),
            *[pltpu.VMEM((2, n_row * size, 128), F32) for size in PIECES],
            *[pltpu.VMEM((2, 64 * size, 128), F32) for size in PIECES],
            pltpu.VMEM((TILE_ROWS, 128), F32),
            pltpu.VMEM((2, 8, 128), F32), pltpu.VMEM((2, n_row, 8, 128), F32), pltpu.VMEM((2, 2, 8, 128), F32),
            pltpu.VMEM(full, F32), pltpu.VMEM(full, F32),
            pltpu.VMEM(full, BF16), pltpu.VMEM(full, BF16), pltpu.VMEM(full, BF16), pltpu.VMEM(full, BF16),
            pltpu.VMEM(full, BF16), pltpu.VMEM(full, BF16),
            dma((2,)), dma((2,)), dma((2, 2)), dma((2,)), dma((2 * n_row,)), dma, dma, dma, dma((2, 2, 2)), dma((2, 2, 2)), dma((2, 3)), dma((2, 3)), dma((2, 3, 2)), dma((2, 3, 2)),
        ],
        compiler_params=pltpu.CompilerParams(
            collective_id=0, has_side_effects=True, vmem_limit_bytes=32 * 1024 * 1024),
    )(pltpu.with_memory_space_constraint(plan, pltpu.HBM), pltpu.with_memory_space_constraint(snapshots, pltpu.HBM))
    return pl.pallas_call(
        deliver,
        out_shape=jax.ShapeDtypeStruct((512, 1, width), F32),
        in_specs=[pl.BlockSpec(memory_space=pl.ANY)],
        out_specs=pl.BlockSpec(memory_space=pltpu.HBM),
        scratch_shapes=[dma],
        compiler_params=pltpu.CompilerParams(vmem_limit_bytes=4 * 1024 * 1024),
    )(result)


def solution(mesh):
    n_row = mesh.shape["row"]
    return jax.shard_map(
        functools.partial(on_device, n_row), mesh=mesh,
        in_specs=(P("row", "pair", None), P()), out_specs=P(None, "pair", "row"), check_vma=False)
```
